128 devices in a mesh: row: 8 (over x, core), col: 16 (over y, z).
Axes of the slice: x: 4, y: 4, z: 4, core: 2. Of those that a mesh axis runs over, the one named last changes fastest.
Arguments:
- filtered: float32 [32768, 2048], P(('row', 'col')), as said below
- hamiltonian_applied: float32 [32768, 2048], P(('row', 'col')), as said below
- rotation: float32 [2048, 2048], replicated, may hold values from -0.125 to 0.125
Outputs:
- intersection: float32 [2048, 2048], P('row', 'col')
- projected: float32 [2048, 2048], P('row', 'col')
- rotated: float32 [32768, 2048], P(('row', 'col'))
The draws below stay inside these ranges and needn't reach their ends.
Inputs may be any that keep to these rules, and one draw needn't show every extreme that they name: `filtered`: finite real values. `hamiltonian_applied`: finite real values.
All inputs are finite; a program needn't handle non-finite values.
Results may differ from the reference program's by a relative error of at most 0.00005.
Values sent between devices are 32-bit elements; how exact they have to be, the bound alone decides.
A program may use at most 192 MiB of HBM per device.

```python
import math
import jax
import jax.numpy as jnp
from jax import lax

M = 2048
GRID = 32768


def orbital_parts(key):
    subkeys = jax.random.split(key, 6)
    row_scale = jnp.exp(jax.random.uniform(subkeys[0], (GRID, 1), jnp.float32, 0.0, math.log(10.0)))
    column_scale = jnp.exp(jax.random.uniform(subkeys[1], (1, M), jnp.float32, math.log(0.4), math.log(4.0)))
    noise = jax.random.normal(subkeys[2], (GRID, M), jnp.float32)
    orbitals = noise * row_scale * column_scale / math.sqrt(21.5)
    energy = jax.random.uniform(subkeys[4], (1, M), jnp.float32, -2.0, 2.0)
    extra = jax.random.normal(subkeys[5], (GRID, M), jnp.float32) * row_scale / math.sqrt(21.5)
    images = energy * orbitals + 0.5 * extra
    return (orbitals, images)


def draw_filtered(key, part):
    return orbital_parts(jax.random.fold_in(key, 11))[0]


def draw_hamiltonian_applied(key, part):
    return orbital_parts(jax.random.fold_in(key, 11))[1]


def bell_draw(key, shape, scale, bound, kind=jnp.bfloat16):
    array = scale * jax.random.normal(key, shape, jnp.float32)
    return jnp.clip(array, min=-bound, max=bound).astype(kind)


def setup_inputs(seed: int = 0) -> dict:
    key_list = jax.random.split(jax.random.key(seed), 4)
    filtered = draw_filtered(jax.random.fold_in(key_list[3], 71), 0)
    hamiltonian_applied = draw_hamiltonian_applied(jax.random.fold_in(key_list[3], 71), 0)
    rotation = bell_draw(key_list[2], (M, M), M ** -0.5, 0.125, jnp.float32)
    return {"filtered": filtered, "hamiltonian_applied": hamiltonian_applied, "rotation": rotation}


def reference(filtered, hamiltonian_applied, rotation):
    scale = 1.0 / GRID
    intersection = jnp.einsum("gi,gj->ij", filtered, filtered, precision=lax.Precision.HIGHEST, preferred_element_type=jnp.float32) * scale
    projected = jnp.einsum("gi,gj->ij", filtered, hamiltonian_applied, precision=lax.Precision.HIGHEST, preferred_element_type=jnp.float32) * scale
    rotated = jnp.dot(filtered, rotation, precision=lax.Precision.HIGHEST, preferred_element_type=jnp.float32)
    return intersection, projected, rotated
```

```python
import jax
import jax.numpy as jnp
from jax import lax
from jax.experimental import pallas as pl
from jax.experimental.pallas import tpu as pltpu
from jax.sharding import PartitionSpec as P

MESH = pl.DeviceIdType.MESH
F32 = jnp.float32
BF16 = jnp.bfloat16
ROWS = 256
M = 2048
TILE = 128
BAND = 144
EARLY = 2
CHUNK = 256


def split(value):
    high = value.astype(BF16)
    low = (value - high.astype(F32)).astype(BF16)
    return high, low


def dot(first, second):
    return jnp.dot(first, second, preferred_element_type=F32)


def dot3(first_high, first_low, second_high, second_low):
    return dot(first_high, second_high) + dot(first_high, second_low) + dot(first_low, second_high)


class Ring:
    def __init__(self, block, landing, send, recv, me, right, left):
        def copy(m):
            source, device = self.routes[m]
            return pltpu.make_async_remote_copy(
                src_ref=source,
                dst_ref=landing(m),
                send_sem=send(m),
                recv_sem=recv(m),
                device_id=device,
                device_id_type=MESH,
            )

        opposite, after, before = (lax.rem(me + n, 4) for n in (2, 1, 3))
        self.after, self.before = block(after, 0), block(before, 1)
        self.landing = landing
        self.mine = (block(me, 0), block(me, 1))
        self.copy = copy
        self.routes = (
            (block(opposite, 0), right),
            (block(opposite, 1), left),
            (block(after, 1), right),
            (block(before, 0), left),
            (self.after, right),
            (self.before, left),
        )

    def start(self, *messages):
        for m in messages:
            self.copy(m).start()

    def forward(self):
        self.copy(0).wait_recv()
        self.after[...] = self.after[...] + self.landing(0)[...]
        self.copy(4).start()
        self.copy(1).wait_recv()
        self.before[...] = self.before[...] + self.landing(1)[...]
        self.copy(5).start()

    def total(self, half):
        left, right = ((4, 3), (2, 5))[half]
        self.copy(left).wait_recv()
        self.copy(right).wait_recv()
        return self.mine[half][...] + self.landing(left)[...] + self.landing(right)[...]

    def drain(self):
        for m in range(6):
            self.copy(m).wait_send()


def kernel(
    psi_hbm, ham_hbm, rot_hbm, over_ref, proj_ref, rotated_hbm,
    raw_a, raw_b, pair_a, pair_b, ah, al, bh, bl, ath, atl,
    rot_buf, out_buf,
    da, db, dc, xa1, xb1, xc1, ea, eb, ec, xa2, xb2, xc2, fa, fb, fc, xa3, xb3, xc3, piece, final,
    sa1, ra1, sb1, rb1, sc1, rc1, s2, r2, s3, r3, s_pair, r_pair, s_fin, r_fin, load_sem, rot_sem, out_sem,
):
    row, col = lax.axis_index("row"), lax.axis_index("col")
    x, core = row // 2, lax.rem(row, 2)
    y, z = col // 4, lax.rem(col, 4)

    def chip(dx=0, dy=0, dz=0):
        return (
            2 * lax.rem(x + dx, 4) + core,
            4 * lax.rem(y + dy, 4) + lax.rem(z + dz, 4),
        )

    partner = (2 * x + 1 - core, col)
    x_right, x_left = chip(dx=1), chip(dx=3)
    y_right, y_left = chip(dy=1), chip(dy=3)
    z_right, z_left = chip(dz=1), chip(dz=3)

    barrier = pltpu.get_barrier_semaphore()
    for device in (partner, x_right, x_left, y_right, y_left, z_right, z_left):
        pl.semaphore_signal(barrier, inc=1, device_id=device, device_id_type=MESH)

    load_a = pltpu.make_async_copy(psi_hbm, raw_a, load_sem.at[0])
    load_b = pltpu.make_async_copy(ham_hbm, raw_b, load_sem.at[1])
    load_a.start()
    load_b.start()

    def rot_load(n):
        slot = lax.rem(n, 2)
        columns = pl.ds(pl.multiple_of(n * CHUNK, CHUNK), CHUNK)
        return pltpu.make_async_copy(rot_hbm.at[:, columns], rot_buf.at[slot], rot_sem.at[slot])

    def rotated_store(n):
        slot = lax.rem(n, 2)
        columns = pl.ds(pl.multiple_of(n * CHUNK, CHUNK), CHUNK)
        return pltpu.make_async_copy(out_buf.at[slot], rotated_hbm.at[:, columns], out_sem.at[slot])

    rot_load(0).start()
    rot_load(1).start()
    pl.semaphore_wait(barrier, 7)

    def pair_copy(source, target, n):
        return pltpu.make_async_remote_copy(
            src_ref=source,
            dst_ref=target,
            send_sem=s_pair.at[n],
            recv_sem=r_pair.at[n],
            device_id=partner,
            device_id_type=MESH,
        )

    pairs = [pair_copy(psi_hbm, pair_a, 0), pair_copy(ham_hbm, pair_b, 1)]
    for copy in pairs:
        copy.start()

    def prepare(raw, high, low, base):
        @pl.loop(0, 8)
        def _(j):
            columns = pl.ds(pl.multiple_of(j * 256, 256), 256)
            h, l = split(raw[:, columns])
            high[base : base + ROWS, columns] = h
            low[base : base + ROWS, columns] = l

    def turn(raw, base):
        @pl.loop(0, 4)
        def _(block):
            start = (2 * block + core) * 256
            h, l = split(raw[:, pl.ds(pl.multiple_of(start, 256), 256)].T)
            ath[block, :, base : base + ROWS] = h
            atl[block, :, base : base + ROWS] = l

    load_a.wait()
    prepare(raw_a, ah, al, 0)
    turn(raw_a, 0)
    load_b.wait()
    prepare(raw_b, bh, bl, 0)

    def rotated_chunk(n):
        slot = lax.rem(n, 2)
        rot_load(n).wait()
        acc = jnp.zeros((ROWS, CHUNK), F32)
        for k in range(8):
            h, l = split(rot_buf[slot, 256 * k : 256 * k + 256, :])
            cut = slice(256 * k, 256 * k + 256)
            acc = acc + dot3(ah[0:ROWS, cut], al[0:ROWS, cut], h, l)

        @pl.when(n >= 2)
        def _():
            rotated_store(n - 2).wait()

        out_buf[slot] = acc
        rotated_store(n).start()

        @pl.when(n + 2 < M // CHUNK)
        def _():
            rot_load(n + 2).start()

    pl.loop(0, EARLY)(rotated_chunk)

    pairs[0].wait_recv()
    prepare(pair_a, ah, al, ROWS)
    turn(pair_a, ROWS)
    pairs[1].wait_recv()
    prepare(pair_b, bh, bl, ROWS)

    y_off = ((2, 1), (3, 0))

    def ring_a1(s):
        return Ring(
            lambda u, h: da.at[u, lax.rem(y + y_off[s][h], 4)],
            lambda m: xa1.at[s, m],
            lambda m: sa1.at[s, m],
            lambda m: ra1.at[s, m],
            x, x_right, x_left,
        )

    def block_of(step):
        return lax.rem(x + 2 + 3 * step + 3 * (step // 2) + 2 * (step // 3), 4)

    def ring_b1(step):
        block = block_of(step)
        return Ring(
            lambda u, h: db.at[block, u, 2 * h : 2 * h + 2],
            lambda m: xb1.at[step, m],
            lambda m: sb1.at[step, m],
            lambda m: rb1.at[step, m],
            y, y_right, y_left,
        )

    def ring_c1(step):
        block = block_of(step)
        return Ring(
            lambda u, h: dc.at[block, u, 2 * h : 2 * h + 2],
            lambda m: xc1.at[step, m],
            lambda m: sc1.at[step, m],
            lambda m: rc1.at[step, m],
            z, z_right, z_left,
        )

    a_rings = [ring_a1(0), ring_a1(1)]

    @pl.loop(0, 4)
    def _(step):
        block = block_of(step)
        strip = 2 * block + core
        b_ring, c_ring = ring_b1(step), ring_c1(step)
        for i, off in enumerate((2, 1, 3, 0)):
            yy = lax.rem(y + off, 4)
            columns = pl.ds(pl.multiple_of(yy * 512, 512), 512)
            acc = dot3(ath[block], atl[block], bh[:, columns], bl[:, columns])
            for t in range(4):
                da[block, yy, t] = acc[0:TILE, TILE * t : TILE * t + TILE]
                db[block, yy, t] = acc[TILE:ROWS, TILE * t : TILE * t + TILE]
            s, h = i // 2, i % 2

            @pl.when(step == 0)
            def _():
                a_rings[s].start(h)

            if h == 1:

                @pl.when(step == 1)
                def _():
                    a_rings[s].start(2)
            else:

                @pl.when(step == 2)
                def _():
                    a_rings[s].start(3)

            if i == 0:
                b_ring.start(0, 1)
            elif i == 1:
                b_ring.start(2)
            elif i == 2:
                b_ring.start(3)
            if i == 0:
                for j in range(5):
                    start = lax.rem(strip + j, 8) * 256
                    columns = pl.ds(pl.multiple_of(start, 256), 256)
                    acc = dot3(ath[block], atl[block], ah[:, columns], al[:, columns])
                    if j < 4:
                        tiles = [(2 * j, acc[:, 0:TILE]), (2 * j + 1, acc[:, TILE:256])]
                    else:
                        swap = strip >= 4
                        top = jnp.where(swap, acc[0:TILE, TILE:256], acc[0:TILE, 0:TILE])
                        low = jnp.where(swap, acc[TILE:ROWS, 0:TILE], acc[TILE:ROWS, TILE:256])
                        tiles = [(8, jnp.concatenate([top, low], axis=0))]
                    for t, tile in tiles:
                        dc[block, :, :, 16 * t : 16 * t + 16, :] = tile.reshape(4, 4, 16, TILE)
                c_ring.start(0, 1, 2, 3)

        @pl.when(step >= 1)
        def _():
            ring_c1(step - 1).forward()
            ring_b1(step - 1).forward()

    ring_c1(3).forward()
    ring_b1(3).forward()
    for ring in a_rings:
        ring.forward()

    pl.loop(EARLY, M // CHUNK)(rotated_chunk)

    def ring_n(stage, part, block, landing, me, right, left):
        send, recv = (s2, r2) if stage == 2 else (s3, r3)
        return Ring(
            block, lambda m: landing.at[m], lambda m: send.at[part, m], lambda m: recv.at[part, m],
            me, right, left,
        )

    ring_a2 = ring_n(2, 0, lambda u, h: ea.at[u, 2 * h : 2 * h + 2], xa2, y, y_right, y_left)
    ring_b2 = ring_n(2, 1, lambda u, h: eb.at[u, 2 * h : 2 * h + 2], xb2, z, z_right, z_left)
    ring_c2 = ring_n(2, 2, lambda u, h: ec.at[u, 2 * h : 2 * h + 2], xc2, x, x_right, x_left)

    @pl.loop(0, 4)
    def _(step):
        ring = ring_c1(step)
        for h in range(2):
            ec[block_of(step), 2 * h : 2 * h + 2] = ring.total(h)

    ring_c2.start(0, 1, 2, 3)
    for s in range(2):
        for h in range(2):
            ea[lax.rem(y + y_off[s][h], 4)] = a_rings[s].total(h)
    ring_a2.start(0, 1, 2, 3)

    @pl.loop(0, 4)
    def _(step):
        ring = ring_b1(step)
        for h in range(2):
            eb[2 * h : 2 * h + 2, block_of(step)] = ring.total(h)

    ring_b2.start(0, 1, 2, 3)
    for ring in (ring_c2, ring_a2, ring_b2):
        ring.forward()

    half = lambda ref, n: lambda u, h: ref.at[u, n * h : n * h + n]
    ring_a3 = ring_n(3, 0, half(fa, 64), xa3, z, z_right, z_left)
    ring_b3 = ring_n(3, 1, half(fb, 64), xb3, x, x_right, x_left)
    ring_c3 = ring_n(3, 2, half(fc, 72), xc3, y, y_right, y_left)
    for ring, ref, nxt in ((ring_c2, fc, ring_c3), (ring_a2, fa, ring_a3), (ring_b2, fb, ring_b3)):
        for h in range(2):
            ref[2 * h : 2 * h + 2] = ring.total(h)
        nxt.start(0, 1, 2, 3)
    for ring in (ring_c3, ring_a3, ring_b3):
        ring.forward()

    for h in range(2):
        piece[72 * h : 72 * h + 72] = ring_c3.total(h)
    scale = 1.0 / (ROWS * 128)
    strip = row
    part = 4 * z + y
    part_half, part_rest = part // 8, lax.rem(part, 8)
    slot = pl.ds(pl.multiple_of(16 * part_rest, 16), 16)
    remote, local = [], []
    for t in range(9):
        other = lax.rem(strip + t // 2, 8)
        side = t % 2 if t < 8 else lax.rem(part_half + strip // 4, 2)
        source = piece.at[16 * t : 16 * t + 16]
        target = 2 * other + side

        def fin(n, device, place):
            return pltpu.make_async_remote_copy(
                src_ref=source,
                dst_ref=place,
                send_sem=s_fin.at[n],
                recv_sem=r_fin.at[0],
                device_id=device,
                device_id_type=MESH,
            )

        direct = fin(t, (strip, target), final.at[part_half, slot])
        stay = pltpu.make_async_copy(source, final.at[part_half, slot], r_fin.at[0])
        pl.when(target != col)(direct.start)
        pl.when(target == col)(stay.start)
        local.append((target, direct))
        if t >= 2:
            mirror = fin(7 + t, (other, 2 * strip + part_half), final.at[side, slot])
            mirror.start()
            remote.append(mirror)

    for ring, base in ((ring_a3, 0), (ring_b3, TILE)):
        for h in range(2):
            proj_ref[base + 64 * h : base + 64 * h + 64, :] = ring.total(h) * scale

    pltpu.make_async_copy(final, final, r_fin.at[0]).wait()
    other, side = col // 2, lax.rem(col, 2)
    distance = lax.rem(other - strip + 8, 8)
    for h in range(2):
        straight = (distance < 4) | ((distance == 4) & (lax.rem(side + strip // 4, 2) == h))
        tile = final[h]
        over_ref[TILE * h : TILE * h + TILE, :] = jnp.where(straight, tile, tile.T) * scale

    for copy in remote:
        copy.wait_send()
    for target, copy in local:
        pl.when(target != col)(copy.wait_send)
    for copy in pairs:
        copy.wait_send()
    for ring in a_rings:
        ring.drain()

    @pl.loop(0, 4)
    def _(step):
        ring_b1(step).drain()
        ring_c1(step).drain()

    for ring in (ring_a2, ring_b2, ring_c2, ring_a3, ring_b3, ring_c3):
        ring.drain()
    rotated_store(M // CHUNK - 2).wait()
    rotated_store(M // CHUNK - 1).wait()


def local(filtered, hamiltonian_applied, rotation):
    vmem = pltpu.VMEM
    dma = pltpu.SemaphoreType.DMA
    any_spec = pl.BlockSpec(memory_space=pl.ANY)
    vmem_spec = pl.BlockSpec(memory_space=pltpu.VMEM)
    flops = 3 * 2 * ROWS * M * M * 3
    return pl.pallas_call(
        kernel,
        out_shape=(
            jax.ShapeDtypeStruct((256, TILE), F32),
            jax.ShapeDtypeStruct((256, TILE), F32),
            jax.ShapeDtypeStruct((ROWS, M), F32),
        ),
        in_specs=[any_spec] * 3,
        out_specs=(vmem_spec, vmem_spec, any_spec),
        scratch_shapes=[
            vmem((ROWS, M), F32), vmem((ROWS, M), F32), vmem((ROWS, M), F32), vmem((ROWS, M), F32),
            vmem((512, M), BF16), vmem((512, M), BF16), vmem((512, M), BF16), vmem((512, M), BF16),
            vmem((4, 256, 512), BF16), vmem((4, 256, 512), BF16),
            vmem((2, M, CHUNK), F32), vmem((2, ROWS, CHUNK), F32),
            vmem((4, 4, 4, TILE, TILE), F32), vmem((4, 4, 4, TILE, TILE), F32), vmem((4, 4, 4, BAND, TILE), F32),
            vmem((2, 6, 4, TILE, TILE), F32), vmem((4, 6, 2, TILE, TILE), F32), vmem((4, 6, 2, BAND, TILE), F32),
            vmem((4, 4, TILE, TILE), F32), vmem((4, 4, TILE, TILE), F32), vmem((4, 4, BAND, TILE), F32),
            vmem((6, 2, TILE, TILE), F32), vmem((6, 2, TILE, TILE), F32), vmem((6, 2, BAND, TILE), F32),
            vmem((4, TILE, TILE), F32), vmem((4, TILE, TILE), F32), vmem((4, BAND, TILE), F32),
            vmem((6, 64, TILE), F32), vmem((6, 64, TILE), F32), vmem((6, 72, TILE), F32),
            vmem((BAND, TILE), F32), vmem((2, TILE, TILE), F32),
            dma((2, 6)), dma((2, 6)), dma((4, 6)), dma((4, 6)), dma((4, 6)), dma((4, 6)),
            dma((3, 6)), dma((3, 6)), dma((3, 6)), dma((3, 6)),
            dma((2,)), dma((2,)), dma((16,)), dma((1,)), dma((2,)), dma((2,)), dma((2,)),
        ],
        compiler_params=pltpu.CompilerParams(
            collective_id=0, has_side_effects=True, vmem_limit_bytes=62 << 20
        ),
        cost_estimate=pl.CostEstimate(flops=flops, bytes_accessed=24 << 20, transcendentals=0),
    )(filtered, hamiltonian_applied, rotation)


def solution(mesh):
    return jax.shard_map(
        local,
        mesh=mesh,
        in_specs=(P(("row", "col"), None), P(("row", "col"), None), P()),
        out_specs=(P("row", "col"), P("row", "col"), P(("row", "col"), None)),
        check_vma=False,
    )
```

```python
import jax
import jax.numpy as jnp
from jax import lax
from jax.experimental import pallas as pl
from jax.experimental.pallas import tpu as pltpu
from jax.sharding import PartitionSpec as P

MESH = pl.DeviceIdType.MESH
F32 = jnp.float32
BF16 = jnp.bfloat16
ROWS = 256
M = 2048
TILE = 128
BAND = 136
CUTS = ((0, 72), (72, 64))
OPENINGS = ((0, 1), (2,), (3,), ())
HALF = (0, 1, 1, 0, 0, 1)
CHUNK = 256


def split(value):
    high = value.astype(BF16)
    low = (value - high.astype(F32)).astype(BF16)
    return high, low


def dot(first, second):
    return jnp.dot(first, second, preferred_element_type=F32)


def dot3(first_high, first_low, second_high, second_low):
    first = jnp.concatenate([first_high, first_high, first_low], axis=1)
    return dot(first, jnp.concatenate([second_high, second_low, second_high], axis=0))


class Ring:
    def __init__(self, block, landing, send, recv, me, right, left):
        def copy(m):
            source, device = self.routes[m]
            return pltpu.make_async_remote_copy(
                src_ref=source,
                dst_ref=landing(m),
                send_sem=send(m),
                recv_sem=recv(m),
                device_id=device,
                device_id_type=MESH,
            )

        opposite, after, before = (lax.rem(me + n, 4) for n in (2, 1, 3))
        self.after, self.before = block(after, 0), block(before, 1)
        self.landing = landing
        self.mine = (block(me, 0), block(me, 1))
        self.copy = copy
        self.routes = (
            (block(opposite, 0), right),
            (block(opposite, 1), left),
            (block(after, 1), right),
            (block(before, 0), left),
            (self.after, right),
            (self.before, left),
        )

    def start(self, *messages):
        for m in messages:
            self.copy(m).start()

    def forward_right(self):
        self.copy(0).wait_recv()
        self.after[...] = self.after[...] + self.landing(0)[...]
        self.copy(4).start()

    def forward_left(self):
        self.copy(1).wait_recv()
        self.before[...] = self.before[...] + self.landing(1)[...]
        self.copy(5).start()

    def forward(self):
        self.forward_right()
        self.forward_left()

    def total(self, half):
        left, right = ((4, 3), (2, 5))[half]
        self.copy(left).wait_recv()
        self.copy(right).wait_recv()
        return self.mine[half][...] + self.landing(left)[...] + self.landing(right)[...]

    def drain(self):
        for m in range(6):
            self.copy(m).wait_send()


def kernel(
    psi_hbm, ham_hbm, rot_hbm, over_ref, proj_ref, rotated_hbm,
    raw_a, raw_b, pair_a, pair_b, ah, al, bh, bl, ath, atl,
    rot_buf, out_buf,
    da, db, dc, xa1, xb1, xc1, ea, eb, ec, xa2, xb2, xc2, fa, fb, fc, xa3, xb3, xc3, piece, final,
    sa1, ra1, sb1, rb1, sc1, rc1, s2, r2, s_pair, r_pair, s_fin, r_fin, load_sem, rot_sem, out_sem,
):
    row, col = lax.axis_index("row"), lax.axis_index("col")
    x, core = row // 2, lax.rem(row, 2)
    y, z = col // 4, lax.rem(col, 4)

    def chip(dx=0, dy=0, dz=0):
        return (
            2 * lax.rem(x + dx, 4) + core,
            4 * lax.rem(y + dy, 4) + lax.rem(z + dz, 4),
        )

    partner = (2 * x + 1 - core, col)
    x_right, x_left = chip(dx=1), chip(dx=3)
    y_right, y_left = chip(dy=1), chip(dy=3)
    z_right, z_left = chip(dz=1), chip(dz=3)

    load_a = pltpu.make_async_copy(psi_hbm, raw_a, load_sem.at[0])
    load_b = pltpu.make_async_copy(ham_hbm, raw_b, load_sem.at[1])
    load_a.start()
    load_b.start()
    barrier = pltpu.get_barrier_semaphore()
    for device in (partner, x_right, x_left, y_right, y_left, z_right, z_left):
        pl.semaphore_signal(barrier, inc=1, device_id=device, device_id_type=MESH)

    def rot_load(n):
        slot = lax.rem(n, 2)
        columns = pl.ds(pl.multiple_of(n * CHUNK, CHUNK), CHUNK)
        return pltpu.make_async_copy(rot_hbm.at[:, columns], rot_buf.at[slot], rot_sem.at[slot])

    def rotated_store(n):
        slot = lax.rem(n, 2)
        columns = pl.ds(pl.multiple_of(n * CHUNK, CHUNK), CHUNK)
        return pltpu.make_async_copy(out_buf.at[slot], rotated_hbm.at[:, columns], out_sem.at[slot])

    def block_of(step):
        return lax.rem(x + 2 + 3 * step + 3 * (step // 2) + 2 * (step // 3), 4)

    def cut(start, width):
        return pl.ds(pl.multiple_of(start, width), width)

    def prepare(raw, high, low, base, columns):
        h, l = split(raw[:, columns])
        high[base : base + ROWS, columns] = h
        low[base : base + ROWS, columns] = l

    load_a.wait()

    @pl.loop(0, 8)
    def _(j):
        prepare(raw_a, ah, al, 0, cut(j * 256, 256))

    load_b.wait()

    @pl.loop(0, 4)
    def _(j):
        prepare(raw_b, bh, bl, 0, cut(j * 512, 512))

    pl.semaphore_wait(barrier, 7)

    y_order = (2, 1, 3, 0)

    def pair_copy(source, target, columns, n):
        return pltpu.make_async_remote_copy(
            src_ref=source.at[:, columns],
            dst_ref=target.at[:, columns],
            send_sem=s_pair.at[n],
            recv_sem=r_pair.at[n],
            device_id=partner,
            device_id_type=MESH,
        )

    def a_columns(first, j):
        return cut(lax.rem(first + j, 8) * 256, 256)

    def b_columns(i):
        return cut(lax.rem(y + y_order[i], 4) * 512, 512)

    def pair_a_copy(first, j):
        return pair_copy(psi_hbm, pair_a, a_columns(first, j), j)

    def pair_b_copy(i):
        return pair_copy(ham_hbm, pair_b, b_columns(i), 8 + i)

    first = 2 * block_of(0) + core
    theirs = 2 * block_of(0) + 1 - core
    pair_a_copy(theirs, 0).start()
    pair_a_copy(theirs, 4).start()
    pair_b_copy(0).start()
    for j in (1, 2, 3):
        pair_a_copy(theirs, j).start()
    for i in (1, 2, 3):
        pair_b_copy(i).start()
    for j in (5, 6, 7):
        pair_a_copy(theirs, j).start()
    rot_load(0).start()
    rot_load(1).start()

    def take_a(j):
        pair_a_copy(first, j).wait_recv()
        prepare(pair_a, ah, al, ROWS, a_columns(first, j))

    def take_b(i):
        pair_b_copy(i).wait_recv()
        prepare(pair_b, bh, bl, ROWS, b_columns(i))

    def turn(columns):
        for raw, base in ((raw_a, 0), (pair_a, ROWS)):
            h, l = split(raw[:, columns].T)
            ath[:, base : base + ROWS] = h
            atl[:, base : base + ROWS] = l

    def rotated_chunk(n):
        slot = lax.rem(n, 2)
        rot_load(n).wait()
        acc = jnp.zeros((ROWS, CHUNK), F32)
        for k in range(8):
            h, l = split(rot_buf[slot, 256 * k : 256 * k + 256, :])
            part = slice(256 * k, 256 * k + 256)
            acc = acc + dot3(ah[0:ROWS, part], al[0:ROWS, part], h, l)

        @pl.when(n >= 2)
        def _():
            rotated_store(n - 2).wait()

        out_buf[slot] = acc
        rotated_store(n).start()

        @pl.when(n + 2 < M // CHUNK)
        def _():
            rot_load(n + 2).start()

    y_off = ((2, 1), (3, 0))

    def ring_a1(s):
        return Ring(
            lambda u, h: da.at[u, lax.rem(y + y_off[s][h], 4)],
            lambda m: xa1.at[s, m],
            lambda m: sa1.at[s, m],
            lambda m: ra1.at[s, m],
            x, x_right, x_left,
        )

    def ring_b1(step):
        block = block_of(step)
        return Ring(
            lambda u, h: db.at[block, u, 2 * h : 2 * h + 2],
            lambda m: xb1.at[step, m],
            lambda m: sb1.at[step, m],
            lambda m: rb1.at[step, m],
            y, y_right, y_left,
        )

    def ring_c1(step):
        block = block_of(step)
        return Ring(
            lambda u, h: dc.at[block, u, 2 * h : 2 * h + 2],
            lambda m: xc1.at[step, m],
            lambda m: sc1.at[step, m],
            lambda m: rc1.at[step, m],
            z, z_right, z_left,
        )

    a_rings = [ring_a1(0), ring_a1(1)]

    @pl.loop(0, 4)
    def _(step):
        block = block_of(step)
        strip = 2 * block + core
        b_ring, c_ring = ring_b1(step), ring_c1(step)
        opening = step == 0

        def at_opening(*takes):
            @pl.when(opening)
            def _():
                for take, n in takes:
                    take(n)

        def square(j):
            columns = a_columns(strip, j)
            return dot3(ath[...], atl[...], ah[:, columns], al[:, columns])

        def projected(i):
            yy = lax.rem(y + y_order[i], 4)
            columns = b_columns(i)
            acc = dot3(ath[...], atl[...], bh[:, columns], bl[:, columns])
            for t in range(4):
                da[block, yy, t, 0:TILE] = acc[0:TILE, TILE * t : TILE * t + TILE]
                db[block, yy, t, 0:TILE] = acc[TILE:ROWS, TILE * t : TILE * t + TILE]
            s, h = i // 2, i % 2

            @pl.when(step == 0)
            def _():
                a_rings[s].start(h)

            @pl.when(step == 2 - h)
            def _():
                a_rings[s].start(3 - h)

        at_opening((take_a, 0))
        turn(a_columns(strip, 0))
        at_opening((take_a, 4))
        acc = square(4)
        swap = strip >= 4
        top = jnp.where(swap, acc[0:TILE, TILE:256], acc[0:TILE, 0:TILE]).reshape(2, 4, 16, TILE)
        low = jnp.where(swap, acc[TILE:ROWS, 0:TILE], acc[TILE:ROWS, TILE:256]).reshape(2, 4, 16, TILE)
        for zz in range(4):
            tile = (top, low)[zz // 2][zz % 2]
            da[block, :, zz, TILE:BAND, :] = tile[:, 0:8]
            db[block, :, zz, TILE:BAND, :] = tile[:, 8:16]
        at_opening((take_b, 0))
        projected(0)
        b_ring.start(0, 1)
        at_opening((take_a, 1), (take_a, 2), (take_a, 3))
        for j in range(4):
            acc = square(j)
            for h in range(2):
                t = 2 * j + h
                tile = acc[:, TILE * h : TILE * h + TILE].reshape(4, 4, 16, TILE)
                dc[block, :, :, 16 * t : 16 * t + 16, :] = tile
        c_ring.start(0, 1, 2, 3)
        at_opening((take_b, 1))
        projected(1)
        b_ring.start(2)
        at_opening((take_b, 2))
        projected(2)
        b_ring.start(3)
        at_opening((take_b, 3))
        projected(3)
        at_opening((take_a, 5), (take_a, 6), (take_a, 7))

        @pl.when(step >= 1)
        def _():
            ring_c1(step - 1).forward()
            ring_b1(step - 1).forward()

        @pl.when(step == 2)
        def _():
            a_rings[0].forward()

    def ring_n(block, landing, sems, me, right, left):
        send, recv = sems
        return Ring(block, landing, lambda m: send.at[m], lambda m: recv.at[m], me, right, left)

    def sems(n):
        return s2.at[n], r2.at[n]

    def in_band(ref, *index):
        return lambda u, h: ref.at[(*index, u, pl.ds(*CUTS[h]))]

    def band_landing(ref, *index):
        return lambda m: ref.at[(*index, m, pl.ds(0, CUTS[HALF[m]][1]))]

    ring_a2 = ring_n(lambda u, h: ea.at[u, 2 * h : 2 * h + 2], lambda m: xa2.at[m], sems(0), y, y_right, y_left)
    ring_c2 = ring_n(lambda u, h: ec.at[u, 2 * h : 2 * h + 2], lambda m: xc2.at[m], sems(1), x, x_right, x_left)
    b2_rings = [
        ring_n(in_band(eb, n), band_landing(xb2, n), sems(2 + n), z, z_right, z_left) for n in range(4)
    ]
    ring_a3 = ring_n(in_band(fa), band_landing(xa3), sems(6), z, z_right, z_left)
    ring_b3 = ring_n(in_band(fb), band_landing(xb3), sems(7), x, x_right, x_left)
    ring_c3 = ring_n(
        lambda u, h: fc.at[u, 64 * h : 64 * h + 64], lambda m: xc3.at[m], sems(8), y, y_right, y_left
    )

    def total_b1(n):
        ring = ring_b1(n)
        for h in range(2):
            eb[n, 2 * h : 2 * h + 2] = ring.total(h)
        b2_rings[n].start(0, 1, 2, 3)

    def total_c1(n):
        ring = ring_c1(n)
        for h in range(2):
            ec[block_of(n), 2 * h : 2 * h + 2] = ring.total(h)
        ring_c2.start(*OPENINGS[n])

    def total_a1(s, h):
        ea[lax.rem(y + y_off[s][h], 4)] = a_rings[s].total(h)
        ring_a2.start(*OPENINGS[2 * s + h])

    def total_b2(n):
        for h in range(2):
            start, size = CUTS[h]
            fb[block_of(n), start : start + size] = b2_rings[n].total(h)
        ring_b3.start(*OPENINGS[n])

    def total_2(ring, ref, then):
        for h in range(2):
            ref[2 * h : 2 * h + 2] = ring.total(h)
        then.start(0, 1, 2, 3)

    def total_c3():
        for h in range(2):
            piece[64 * h : 64 * h + 64] = ring_c3.total(h)
        for finish in finishes[:8]:
            finish.start()

    def total_3(ring, base, rest):
        head, tail = ring.total(0), ring.total(1)
        proj_ref[base : base + 72, :] = head * scale
        proj_ref[base + 72 : base + TILE, :] = tail[0:56] * scale
        piece[rest : rest + 8] = tail[56:64]

    scale = 1.0 / (ROWS * 128)
    strip = row
    part = 4 * z + y
    part_half, part_rest = part // 8, lax.rem(part, 8)
    slot = pl.ds(pl.multiple_of(16 * part_rest, 16), 16)

    class Finish:
        def __init__(self, t):
            self.t, self.source = t, piece.at[16 * t : 16 * t + 16]
            self.other = lax.rem(strip + t // 2, 8)
            self.side = t % 2 if t < 8 else lax.rem(part_half + strip // 4, 2)
            self.target = 2 * self.other + self.side

        def copy(self, n, device, place):
            return pltpu.make_async_remote_copy(
                src_ref=self.source,
                dst_ref=place,
                send_sem=s_fin.at[n],
                recv_sem=r_fin.at[0],
                device_id=device,
                device_id_type=MESH,
            )

        def direct(self):
            return self.copy(self.t, (strip, self.target), final.at[part_half, slot])

        def mirror(self):
            return self.copy(7 + self.t, (self.other, 2 * strip + part_half), final.at[self.side, slot])

        def start(self):
            stay = pltpu.make_async_copy(self.source, final.at[part_half, slot], r_fin.at[0])
            direct = self.direct()
            pl.when(self.target != col)(direct.start)
            pl.when(self.target == col)(stay.start)
            if self.t >= 2:
                self.mirror().start()

        def drain(self):
            pl.when(self.target != col)(self.direct().wait_send)
            if self.t >= 2:
                self.mirror().wait_send()

    finishes = [Finish(t) for t in range(9)]

    a_rings[1].forward_right()
    total_b1(0)
    total_c1(0)
    a_rings[1].forward_left()
    pl.loop(0, 2)(rotated_chunk)
    total_c1(1)
    total_b1(1)
    pl.loop(2, 3)(rotated_chunk)
    ring_c1(3).forward_left()
    ring_b1(3).forward_right()
    ring_c1(3).forward_right()
    ring_b1(3).forward_left()
    pl.loop(3, 4)(rotated_chunk)
    total_a1(0, 0)
    pl.loop(4, 6)(rotated_chunk)
    total_b1(2)
    total_c1(2)
    b2_rings[0].forward_right()
    b2_rings[1].forward_left()
    b2_rings[1].forward_right()
    ring_c2.forward_left()
    b2_rings[0].forward_left()
    total_a1(1, 0)
    total_b1(3)
    total_a1(0, 1)
    pl.loop(6, 7)(rotated_chunk)
    b2_rings[2].forward_right()
    ring_a2.forward_right()
    b2_rings[2].forward_left()
    ring_a2.forward_left()
    ring_c2.forward_right()
    total_c1(3)
    pl.loop(7, 8)(rotated_chunk)
    b2_rings[3].forward_left()
    b2_rings[3].forward_right()
    total_b2(0)
    total_b2(1)
    total_a1(1, 1)
    total_b2(2)
    total_b2(3)
    total_2(ring_a2, fa, ring_a3)
    total_2(ring_c2, fc, ring_c3)
    ring_b3.forward_left()
    ring_b3.forward_right()
    ring_a3.forward_left()
    ring_a3.forward_right()
    ring_c3.forward_right()
    ring_c3.forward_left()
    total_3(ring_b3, TILE, 136)
    total_3(ring_a3, 0, 128)
    finishes[8].start()
    total_c3()

    for n in range(12):
        (pair_a_copy(theirs, n) if n < 8 else pair_b_copy(n - 8)).wait_send()
    for ring in a_rings:
        ring.drain()

    @pl.loop(0, 4)
    def _(step):
        ring_b1(step).drain()
        ring_c1(step).drain()

    for ring in (ring_a2, ring_c2, *b2_rings, ring_a3, ring_b3, ring_c3):
        ring.drain()
    rotated_store(M // CHUNK - 2).wait()
    rotated_store(M // CHUNK - 1).wait()

    pltpu.make_async_copy(final, final, r_fin.at[0]).wait()
    other, side = col // 2, lax.rem(col, 2)
    distance = lax.rem(other - strip + 8, 8)
    for h in range(2):
        straight = (distance < 4) | ((distance == 4) & (lax.rem(side + strip // 4, 2) == h))
        tile = final[h]
        over_ref[TILE * h : TILE * h + TILE, :] = jnp.where(straight, tile, tile.T) * scale
    for finish in finishes:
        finish.drain()


def hand_on(over_in, proj_in, rotated_in, over_out, proj_out, rotated_out, over, proj, rotated, load, store):
    moves = [(over_in, over, over_out), (proj_in, proj, proj_out)]
    for n in range(4):
        rows = pl.ds(64 * n, 64)
        moves.append((rotated_in.at[rows], rotated.at[rows], rotated_out.at[rows]))
    loads = [pltpu.make_async_copy(a, b, load.at[n]) for n, (a, b, _) in enumerate(moves)]
    stores = [pltpu.make_async_copy(b, c, store.at[n]) for n, (_, b, c) in enumerate(moves)]
    for copy in loads:
        copy.start()
    for first, second in zip(loads, stores):
        first.wait()
        second.start()
    for copy in stores:
        copy.wait()


def local(filtered, hamiltonian_applied, rotation):
    vmem = pltpu.VMEM
    dma = pltpu.SemaphoreType.DMA
    any_spec = pl.BlockSpec(memory_space=pl.ANY)
    vmem_spec = pl.BlockSpec(memory_space=pltpu.VMEM)
    flops = 3 * 2 * ROWS * M * M * 3
    shapes = (
        jax.ShapeDtypeStruct((256, TILE), F32),
        jax.ShapeDtypeStruct((256, TILE), F32),
        jax.ShapeDtypeStruct((ROWS, M), F32),
    )
    made = pl.pallas_call(
        kernel,
        out_shape=shapes,
        in_specs=[any_spec] * 3,
        out_specs=(vmem_spec, vmem_spec, any_spec),
        scratch_shapes=[
            vmem((ROWS, M), F32), vmem((ROWS, M), F32), vmem((ROWS, M), F32), vmem((ROWS, M), F32),
            vmem((512, M), BF16), vmem((512, M), BF16), vmem((512, M), BF16), vmem((512, M), BF16),
            vmem((256, 512), BF16), vmem((256, 512), BF16),
            vmem((2, M, CHUNK), F32), vmem((2, ROWS, CHUNK), F32),
            vmem((4, 4, 4, BAND, TILE), F32), vmem((4, 4, 4, BAND, TILE), F32), vmem((4, 4, 4, TILE, TILE), F32),
            vmem((2, 6, 4, BAND, TILE), F32), vmem((4, 6, 2, BAND, TILE), F32), vmem((4, 6, 2, TILE, TILE), F32),
            vmem((4, 4, BAND, TILE), F32), vmem((4, 4, BAND, TILE), F32), vmem((4, 4, TILE, TILE), F32),
            vmem((6, 2, BAND, TILE), F32), vmem((4, 6, 72, TILE), F32), vmem((6, 2, TILE, TILE), F32),
            vmem((4, BAND, TILE), F32), vmem((4, BAND, TILE), F32), vmem((4, TILE, TILE), F32),
            vmem((6, 72, TILE), F32), vmem((6, 72, TILE), F32), vmem((6, 64, TILE), F32),
            vmem((144, TILE), F32), vmem((2, TILE, TILE), F32),
            dma((2, 6)), dma((2, 6)), dma((4, 6)), dma((4, 6)), dma((4, 6)), dma((4, 6)),
            dma((9, 6)), dma((9, 6)),
            dma((12,)), dma((12,)), dma((16,)), dma((1,)), dma((2,)), dma((2,)), dma((2,)),
        ],
        compiler_params=pltpu.CompilerParams(
            collective_id=0, has_side_effects=True, vmem_limit_bytes=62 << 20
        ),
        cost_estimate=pl.CostEstimate(flops=flops, bytes_accessed=24 << 20, transcendentals=0),
    )(filtered, hamiltonian_applied, rotation)
    return pl.pallas_call(
        hand_on,
        out_shape=shapes,
        in_specs=[any_spec] * 3,
        out_specs=(any_spec,) * 3,
        scratch_shapes=[vmem((256, TILE), F32), vmem((256, TILE), F32), vmem((ROWS, M), F32), dma((6,)), dma((6,))],
    )(*made)


def solution(mesh):
    return jax.shard_map(
        local,
        mesh=mesh,
        in_specs=(P(("row", "col"), None), P(("row", "col"), None), P()),
        out_specs=(P("row", "col"), P("row", "col"), P(("row", "col"), None)),
        check_vma=False,
    )
```

```python
import jax
import jax.numpy as jnp
from jax import lax
from jax.experimental import pallas as pl
from jax.experimental.pallas import tpu as pltpu
from jax.sharding import PartitionSpec as P

MESH = pl.DeviceIdType.MESH
F32 = jnp.float32
BF16 = jnp.bfloat16
ROWS = 256
M = 2048
TILE = 128
BAND = 136
CUTS = ((0, 72), (72, 64))
OPENINGS = ((0, 1), (2,), (3,), ())
HALF = (0, 1, 1, 0, 0, 1)
CHUNK = 256


def split(value):
    high = value.astype(BF16)
    low = (value - high.astype(F32)).astype(BF16)
    return high, low


def dot(first, second):
    return jnp.dot(first, second, preferred_element_type=F32)


def dot3(first_high, first_low, second_high, second_low):
    first = jnp.concatenate([first_high, first_high, first_low], axis=1)
    return dot(first, jnp.concatenate([second_high, second_low, second_high], axis=0))


class Ring:
    def __init__(self, block, landing, send, recv, me, right, left):
        def copy(m):
            source, device = self.routes[m]
            return pltpu.make_async_remote_copy(
                src_ref=source,
                dst_ref=landing(m),
                send_sem=send(m),
                recv_sem=recv(m),
                device_id=device,
                device_id_type=MESH,
            )

        opposite, after, before = (lax.rem(me + n, 4) for n in (2, 1, 3))
        self.after, self.before = block(after, 0), block(before, 1)
        self.landing = landing
        self.mine = (block(me, 0), block(me, 1))
        self.copy = copy
        self.routes = (
            (block(opposite, 0), right),
            (block(opposite, 1), left),
            (block(after, 1), right),
            (block(before, 0), left),
            (self.after, right),
            (self.before, left),
        )

    def start(self, *messages):
        for m in messages:
            self.copy(m).start()

    def forward_right(self):
        self.copy(0).wait_recv()
        self.after[...] = self.after[...] + self.landing(0)[...]
        self.copy(4).start()

    def forward_left(self):
        self.copy(1).wait_recv()
        self.before[...] = self.before[...] + self.landing(1)[...]
        self.copy(5).start()

    def forward(self):
        self.forward_right()
        self.forward_left()

    def total(self, half):
        left, right = ((4, 3), (2, 5))[half]
        self.copy(left).wait_recv()
        self.copy(right).wait_recv()
        return self.mine[half][...] + self.landing(left)[...] + self.landing(right)[...]

    def drain(self):
        for m in range(6):
            self.copy(m).wait_send()


class Direct:
    def __init__(self, block, landing, send, recv, me, devices):
        self.mine, self.landing = block(me), landing

        def copy(m):
            return pltpu.make_async_remote_copy(
                src_ref=block(lax.rem(me + (1, 3, 2)[m], 4)),
                dst_ref=landing(m),
                send_sem=send(m),
                recv_sem=recv(m),
                device_id=devices[m],
                device_id_type=MESH,
            )

        self.copy = copy

    def start(self, *messages):
        for m in messages:
            self.copy(m).start()

    def total(self):
        for m in range(3):
            self.copy(m).wait_recv()
        return (self.mine[...] + self.landing(0)[...]) + (self.landing(1)[...] + self.landing(2)[...])

    def drain(self):
        for m in range(3):
            self.copy(m).wait_send()


def kernel(
    psi_hbm, ham_hbm, rot_hbm, over_ref, proj_ref, rotated_hbm,
    raw_a, raw_b, pair_a, pair_b, ah, al, bh, bl, ath, atl,
    rot_buf, out_buf,
    da, db, dc, xa1, xb1, xc1, ea, eb, ec, xa2, xb2, xb2_last, xc2, fa, fb, fc, xa3, xb3, xc3, piece, final,
    sa1, ra1, sb1, rb1, sc1, rc1, s2, r2, s_pair, r_pair, s_fin, r_fin, load_sem, rot_sem, out_sem,
):
    row, col = lax.axis_index("row"), lax.axis_index("col")
    x, core = row // 2, lax.rem(row, 2)
    y, z = col // 4, lax.rem(col, 4)

    def chip(dx=0, dy=0, dz=0):
        return (
            2 * lax.rem(x + dx, 4) + core,
            4 * lax.rem(y + dy, 4) + lax.rem(z + dz, 4),
        )

    partner = (2 * x + 1 - core, col)
    x_right, x_left = chip(dx=1), chip(dx=3)
    y_right, y_left = chip(dy=1), chip(dy=3)
    z_right, z_left = chip(dz=1), chip(dz=3)

    load_a = pltpu.make_async_copy(psi_hbm, raw_a, load_sem.at[0])
    load_b = pltpu.make_async_copy(ham_hbm, raw_b, load_sem.at[1])
    load_a.start()
    load_b.start()
    barrier = pltpu.get_barrier_semaphore()
    for device in (partner, x_right, x_left, y_right, y_left, z_right, z_left):
        pl.semaphore_signal(barrier, inc=1, device_id=device, device_id_type=MESH)

    def rot_load(n):
        slot = lax.rem(n, 2)
        columns = pl.ds(pl.multiple_of(n * CHUNK, CHUNK), CHUNK)
        return pltpu.make_async_copy(rot_hbm.at[:, columns], rot_buf.at[slot], rot_sem.at[slot])

    def rotated_store(n):
        slot = lax.rem(n, 2)
        columns = pl.ds(pl.multiple_of(n * CHUNK, CHUNK), CHUNK)
        return pltpu.make_async_copy(out_buf.at[slot], rotated_hbm.at[:, columns], out_sem.at[slot])

    def block_of(step):
        return lax.rem(x + 2 + 3 * step + 3 * (step // 2) + 2 * (step // 3), 4)

    def cut(start, width):
        return pl.ds(pl.multiple_of(start, width), width)

    def prepare(raw, high, low, base, columns):
        h, l = split(raw[:, columns])
        high[base : base + ROWS, columns] = h
        low[base : base + ROWS, columns] = l

    load_a.wait()

    @pl.loop(0, 8)
    def _(j):
        prepare(raw_a, ah, al, 0, cut(j * 256, 256))

    load_b.wait()

    @pl.loop(0, 4)
    def _(j):
        prepare(raw_b, bh, bl, 0, cut(j * 512, 512))

    pl.semaphore_wait(barrier, 7)

    y_order = (2, 1, 3, 0)

    def pair_copy(source, target, columns, n):
        return pltpu.make_async_remote_copy(
            src_ref=source.at[:, columns],
            dst_ref=target.at[:, columns],
            send_sem=s_pair.at[n],
            recv_sem=r_pair.at[n],
            device_id=partner,
            device_id_type=MESH,
        )

    def a_columns(first, j):
        return cut(lax.rem(first + j, 8) * 256, 256)

    def b_columns(i):
        return cut(lax.rem(y + y_order[i], 4) * 512, 512)

    def pair_a_copy(first, j):
        return pair_copy(psi_hbm, pair_a, a_columns(first, j), j)

    def pair_b_copy(i):
        return pair_copy(ham_hbm, pair_b, b_columns(i), 8 + i)

    first = 2 * block_of(0) + core
    theirs = 2 * block_of(0) + 1 - core
    pair_a_copy(theirs, 0).start()
    pair_a_copy(theirs, 4).start()
    pair_b_copy(0).start()
    pair_b_copy(1).start()
    for j in (1, 2, 3):
        pair_a_copy(theirs, j).start()
    for i in (2, 3):
        pair_b_copy(i).start()
    for j in (5, 6, 7):
        pair_a_copy(theirs, j).start()
    rot_load(0).start()
    rot_load(1).start()

    def take_a(j):
        pair_a_copy(first, j).wait_recv()
        prepare(pair_a, ah, al, ROWS, a_columns(first, j))

    def take_b(i):
        pair_b_copy(i).wait_recv()
        prepare(pair_b, bh, bl, ROWS, b_columns(i))

    def turn(columns):
        for raw, base in ((raw_a, 0), (pair_a, ROWS)):
            h, l = split(raw[:, columns].T)
            ath[:, base : base + ROWS] = h
            atl[:, base : base + ROWS] = l

    def rotated_chunk(n):
        slot = lax.rem(n, 2)
        rot_load(n).wait()
        acc = jnp.zeros((ROWS, CHUNK), F32)
        for k in range(8):
            h, l = split(rot_buf[slot, 256 * k : 256 * k + 256, :])
            part = slice(256 * k, 256 * k + 256)
            acc = acc + dot3(ah[0:ROWS, part], al[0:ROWS, part], h, l)

        @pl.when(n >= 2)
        def _():
            rotated_store(n - 2).wait()

        out_buf[slot] = acc
        rotated_store(n).start()

        @pl.when(n + 2 < M // CHUNK)
        def _():
            rot_load(n + 2).start()

    y_off = ((2, 1), (3, 0))

    def ring_a1(n):
        s, pair = n // 2, n % 2
        return Ring(
            lambda u, h: da.at[u, lax.rem(y + y_off[s][h], 4), 2 * pair : 2 * pair + 2],
            lambda m: xa1.at[n, m],
            lambda m: sa1.at[n, m],
            lambda m: ra1.at[n, m],
            x, x_right, x_left,
        )

    def ring_b1(step):
        block = block_of(step)
        return Ring(
            lambda u, h: db.at[block, u, 2 * h : 2 * h + 2],
            lambda m: xb1.at[step, m],
            lambda m: sb1.at[step, m],
            lambda m: rb1.at[step, m],
            y, y_right, y_left,
        )

    def ring_c1(step):
        block = block_of(step)
        return Ring(
            lambda u, h: dc.at[block, u, 2 * h : 2 * h + 2],
            lambda m: xc1.at[step, m],
            lambda m: sc1.at[step, m],
            lambda m: rc1.at[step, m],
            z, z_right, z_left,
        )

    a_rings = [ring_a1(n) for n in range(4)]

    @pl.loop(0, 4)
    def _(step):
        block = block_of(step)
        strip = 2 * block + core
        b_ring, c_ring = ring_b1(step), ring_c1(step)
        opening = step == 0

        def at_opening(*takes):
            @pl.when(opening)
            def _():
                for take, n in takes:
                    take(n)

        def square(j):
            columns = a_columns(strip, j)
            return dot3(ath[...], atl[...], ah[:, columns], al[:, columns])

        def projected(i):
            yy = lax.rem(y + y_order[i], 4)
            columns = b_columns(i)
            acc = dot3(ath[...], atl[...], bh[:, columns], bl[:, columns])
            for t in range(4):
                da[block, yy, t, 0:TILE] = acc[0:TILE, TILE * t : TILE * t + TILE]
                db[block, yy, t, 0:TILE] = acc[TILE:ROWS, TILE * t : TILE * t + TILE]
            s, h = i // 2, i % 2

            @pl.when(step == 0)
            def _():
                for ring in a_rings[2 * s : 2 * s + 2]:
                    ring.start(h)

            @pl.when(step == 2 - h)
            def _():
                for ring in a_rings[2 * s : 2 * s + 2]:
                    ring.start(3 - h)

        at_opening((take_a, 0))
        turn(a_columns(strip, 0))
        at_opening((take_a, 4))
        acc = square(4)
        swap = strip >= 4
        top = jnp.where(swap, acc[0:TILE, TILE:256], acc[0:TILE, 0:TILE]).reshape(2, 4, 16, TILE)
        low = jnp.where(swap, acc[TILE:ROWS, 0:TILE], acc[TILE:ROWS, TILE:256]).reshape(2, 4, 16, TILE)
        for zz in range(4):
            tile = (top, low)[zz // 2][zz % 2]
            da[block, :, zz, TILE:BAND, :] = tile[:, 0:8]
            db[block, :, zz, TILE:BAND, :] = tile[:, 8:16]
        at_opening((take_b, 0))
        projected(0)
        b_ring.start(0, 1)
        at_opening((take_b, 1))
        projected(1)
        b_ring.start(2)
        at_opening((take_a, 1), (take_a, 2), (take_a, 3))
        for j in range(4):
            acc = square(j)
            for h in range(2):
                t = 2 * j + h
                tile = acc[:, TILE * h : TILE * h + TILE].reshape(4, 4, 16, TILE)
                dc[block, :, :, 16 * t : 16 * t + 16, :] = tile
        c_ring.start(0, 1, 2, 3)
        at_opening((take_b, 2))
        projected(2)
        b_ring.start(3)
        at_opening((take_b, 3))
        projected(3)
        at_opening((take_a, 5), (take_a, 6), (take_a, 7))

        @pl.when(step >= 1)
        def _():
            ring_c1(step - 1).forward()
            ring_b1(step - 1).forward()

        @pl.when(step == 2)
        def _():
            a_rings[0].forward()
            a_rings[1].forward()

    def ring_n(block, landing, sems, me, right, left):
        send, recv = sems
        return Ring(block, landing, lambda m: send.at[m], lambda m: recv.at[m], me, right, left)

    def sems(n):
        return s2.at[n], r2.at[n]

    def in_band(ref, *index):
        return lambda u, h: ref.at[(*index, u, pl.ds(*CUTS[h]))]

    def band_landing(ref, *index):
        return lambda m: ref.at[(*index, m, pl.ds(0, CUTS[HALF[m]][1]))]

    ring_a2 = ring_n(lambda u, h: ea.at[u, 2 * h : 2 * h + 2], lambda m: xa2.at[m], sems(0), y, y_right, y_left)
    ring_c2 = ring_n(lambda u, h: ec.at[u, 2 * h : 2 * h + 2], lambda m: xc2.at[m], sems(1), x, x_right, x_left)
    b2_rings = [
        ring_n(in_band(eb, n), band_landing(xb2, n), sems(2 + n), z, z_right, z_left) for n in range(3)
    ]

    def direct_n(block, landing, n, me, devices):
        return Direct(block, lambda m: landing.at[m], lambda m: s2.at[n, m], lambda m: r2.at[n, m], me, devices)

    x_devices = (x_right, x_left, chip(dx=2))
    y_devices = (y_right, y_left, chip(dy=2))
    z_devices = (z_right, z_left, chip(dz=2))
    b2_last = direct_n(lambda u: eb.at[3, u], xb2_last, 5, z, z_devices)
    ring_a3 = direct_n(lambda u: fa.at[u], xa3, 6, z, z_devices)
    ring_b3 = direct_n(lambda u: fb.at[u], xb3, 7, x, x_devices)
    ring_c3 = direct_n(lambda u: fc.at[u], xc3, 8, y, y_devices)

    def total_b1(n):
        ring = ring_b1(n)
        for h in range(2):
            eb[n, 2 * h : 2 * h + 2] = ring.total(h)
        if n < 3:
            b2_rings[n].start(0, 1, 2, 3)
        else:
            b2_last.start(2, 0, 1)

    def total_c1(n):
        ring = ring_c1(n)
        for h in range(2):
            ec[block_of(n), 2 * h : 2 * h + 2] = ring.total(h)
        ring_c2.start(*OPENINGS[n])

    def total_a1(s, h):
        for n in range(2):
            ea[lax.rem(y + y_off[s][h], 4), 2 * n : 2 * n + 2] = a_rings[2 * s + n].total(h)
        ring_a2.start(*OPENINGS[2 * s + h])

    def total_b2(n):
        if n == 3:
            fb[block_of(n)] = b2_last.total()
            return
        for h in range(2):
            start, size = CUTS[h]
            fb[block_of(n), start : start + size] = b2_rings[n].total(h)
        ring_b3.start((2, 0, 1)[n])

    def total_2(ring, ref, then):
        for h in range(2):
            ref[2 * h : 2 * h + 2] = ring.total(h)
        then.start(2, 0, 1)

    def total_c3():
        piece[0:TILE] = ring_c3.total()
        for finish in finishes[:8]:
            finish.start()

    def total_3(ring, base, rest):
        total = ring.total()
        proj_ref[base : base + TILE, :] = total[0:TILE] * scale
        piece[rest : rest + 8] = total[TILE:BAND]

    scale = 1.0 / (ROWS * 128)
    strip = row
    part = 4 * z + y
    part_half, part_rest = part // 8, lax.rem(part, 8)
    slot = pl.ds(pl.multiple_of(16 * part_rest, 16), 16)

    class Finish:
        def __init__(self, t):
            self.t, self.source = t, piece.at[16 * t : 16 * t + 16]
            self.other = lax.rem(strip + t // 2, 8)
            self.side = t % 2 if t < 8 else lax.rem(part_half + strip // 4, 2)
            self.target = 2 * self.other + self.side

        def copy(self, n, device, place):
            return pltpu.make_async_remote_copy(
                src_ref=self.source,
                dst_ref=place,
                send_sem=s_fin.at[n],
                recv_sem=r_fin.at[0],
                device_id=device,
                device_id_type=MESH,
            )

        def direct(self):
            return self.copy(self.t, (strip, self.target), final.at[part_half, slot])

        def mirror(self):
            return self.copy(7 + self.t, (self.other, 2 * strip + part_half), final.at[self.side, slot])

        def start(self):
            stay = pltpu.make_async_copy(self.source, final.at[part_half, slot], r_fin.at[0])
            direct = self.direct()
            pl.when(self.target != col)(direct.start)
            pl.when(self.target == col)(stay.start)
            if self.t >= 2:
                self.mirror().start()

        def drain(self):
            pl.when(self.target != col)(self.direct().wait_send)
            if self.t >= 2:
                self.mirror().wait_send()

    finishes = [Finish(t) for t in range(9)]

    a_rings[2].forward_right()
    a_rings[3].forward_right()
    total_c1(0)
    pl.loop(0, 3)(rotated_chunk)
    total_c1(1)
    pl.loop(3, 4)(rotated_chunk)
    ring_b1(3).forward_left()
    ring_b1(3).forward_right()
    ring_c1(3).forward_right()
    a_rings[3].forward_left()
    total_b1(0)
    ring_c1(3).forward_left()
    total_a1(0, 0)
    total_a1(0, 1)
    pl.loop(4, 6)(rotated_chunk)
    total_c1(2)
    total_b1(2)
    ring_c2.forward_left()
    a_rings[2].forward_left()
    total_b1(1)
    b2_rings[0].forward_left()
    total_a1(1, 0)
    pl.loop(6, 7)(rotated_chunk)
    b2_rings[0].forward_right()
    ring_c2.forward_right()
    b2_rings[2].forward_left()
    ring_a2.forward_left()
    ring_a2.forward_right()
    b2_rings[2].forward_right()
    total_c1(3)
    b2_rings[1].forward_left()
    b2_rings[1].forward_right()
    total_b1(3)
    pl.loop(7, 8)(rotated_chunk)
    total_b2(2)
    total_b2(0)
    total_b2(1)
    total_2(ring_c2, fc, ring_c3)
    total_a1(1, 1)
    total_2(ring_a2, fa, ring_a3)
    total_b2(3)
    total_3(ring_b3, TILE, 136)
    total_c3()
    total_3(ring_a3, 0, 128)
    finishes[8].start()

    for n in range(12):
        (pair_a_copy(theirs, n) if n < 8 else pair_b_copy(n - 8)).wait_send()
    for ring in a_rings:
        ring.drain()

    @pl.loop(0, 4)
    def _(step):
        ring_b1(step).drain()
        ring_c1(step).drain()

    for ring in (ring_a2, ring_c2, *b2_rings, b2_last, ring_a3, ring_b3, ring_c3):
        ring.drain()
    rotated_store(M // CHUNK - 2).wait()
    rotated_store(M // CHUNK - 1).wait()

    pltpu.make_async_copy(final, final, r_fin.at[0]).wait()
    other, side = col // 2, lax.rem(col, 2)
    distance = lax.rem(other - strip + 8, 8)
    for h in range(2):
        straight = (distance < 4) | ((distance == 4) & (lax.rem(side + strip // 4, 2) == h))
        tile = final[h]
        over_ref[TILE * h : TILE * h + TILE, :] = jnp.where(straight, tile, tile.T) * scale
    for finish in finishes:
        finish.drain()


def hand_on(over_in, proj_in, rotated_in, over_out, proj_out, rotated_out, over, proj, rotated, load, store):
    moves = [(over_in, over, over_out), (proj_in, proj, proj_out)]
    for n in range(4):
        rows = pl.ds(64 * n, 64)
        moves.append((rotated_in.at[rows], rotated.at[rows], rotated_out.at[rows]))
    loads = [pltpu.make_async_copy(a, b, load.at[n]) for n, (a, b, _) in enumerate(moves)]
    stores = [pltpu.make_async_copy(b, c, store.at[n]) for n, (_, b, c) in enumerate(moves)]
    for copy in loads:
        copy.start()
    for first, second in zip(loads, stores):
        first.wait()
        second.start()
    for copy in stores:
        copy.wait()


def local(filtered, hamiltonian_applied, rotation):
    vmem = pltpu.VMEM
    dma = pltpu.SemaphoreType.DMA
    any_spec = pl.BlockSpec(memory_space=pl.ANY)
    vmem_spec = pl.BlockSpec(memory_space=pltpu.VMEM)
    flops = 3 * 2 * ROWS * M * M * 3
    shapes = (
        jax.ShapeDtypeStruct((256, TILE), F32),
        jax.ShapeDtypeStruct((256, TILE), F32),
        jax.ShapeDtypeStruct((ROWS, M), F32),
    )
    made = pl.pallas_call(
        kernel,
        out_shape=shapes,
        in_specs=[any_spec] * 3,
        out_specs=(vmem_spec, vmem_spec, any_spec),
        scratch_shapes=[
            vmem((ROWS, M), F32), vmem((ROWS, M), F32), vmem((ROWS, M), F32), vmem((ROWS, M), F32),
            vmem((512, M), BF16), vmem((512, M), BF16), vmem((512, M), BF16), vmem((512, M), BF16),
            vmem((256, 512), BF16), vmem((256, 512), BF16),
            vmem((2, M, CHUNK), F32), vmem((2, ROWS, CHUNK), F32),
            vmem((4, 4, 4, BAND, TILE), F32), vmem((4, 4, 4, BAND, TILE), F32), vmem((4, 4, 4, TILE, TILE), F32),
            vmem((4, 6, 2, BAND, TILE), F32), vmem((4, 6, 2, BAND, TILE), F32), vmem((4, 6, 2, TILE, TILE), F32),
            vmem((4, 4, BAND, TILE), F32), vmem((4, 4, BAND, TILE), F32), vmem((4, 4, TILE, TILE), F32),
            vmem((6, 2, BAND, TILE), F32), vmem((3, 6, 72, TILE), F32), vmem((3, BAND, TILE), F32), vmem((6, 2, TILE, TILE), F32),
            vmem((4, BAND, TILE), F32), vmem((4, BAND, TILE), F32), vmem((4, TILE, TILE), F32),
            vmem((3, BAND, TILE), F32), vmem((3, BAND, TILE), F32), vmem((3, TILE, TILE), F32),
            vmem((144, TILE), F32), vmem((2, TILE, TILE), F32),
            dma((4, 6)), dma((4, 6)), dma((4, 6)), dma((4, 6)), dma((4, 6)), dma((4, 6)),
            dma((9, 6)), dma((9, 6)),
            dma((12,)), dma((12,)), dma((16,)), dma((1,)), dma((2,)), dma((2,)), dma((2,)),
        ],
        compiler_params=pltpu.CompilerParams(
            collective_id=0, has_side_effects=True, vmem_limit_bytes=62 << 20
        ),
        cost_estimate=pl.CostEstimate(flops=flops, bytes_accessed=24 << 20, transcendentals=0),
    )(filtered, hamiltonian_applied, rotation)
    return pl.pallas_call(
        hand_on,
        out_shape=shapes,
        in_specs=[any_spec] * 3,
        out_specs=(any_spec,) * 3,
        scratch_shapes=[vmem((256, TILE), F32), vmem((256, TILE), F32), vmem((ROWS, M), F32), dma((6,)), dma((6,))],
    )(*made)


def solution(mesh):
    return jax.shard_map(
        local,
        mesh=mesh,
        in_specs=(P(("row", "col"), None), P(("row", "col"), None), P()),
        out_specs=(P("row", "col"), P("row", "col"), P(("row", "col"), None)),
        check_vma=False,
    )
```

```python
import jax
import jax.numpy as jnp
from jax import lax
from jax.experimental import pallas as pl
from jax.experimental.pallas import tpu as pltpu
from jax.sharding import PartitionSpec as P

MESH = pl.DeviceIdType.MESH
F32 = jnp.float32
BF16 = jnp.bfloat16
ROWS = 256
M = 2048
TILE = 128
BAND = 136
CUTS = ((0, 72), (72, 64))
OPENINGS = ((0, 1), (2,), (3,), ())
HALF = (0, 1, 1, 0, 0, 1)
CHUNK = 256


def split(value):
    high = value.astype(BF16)
    low = (value - high.astype(F32)).astype(BF16)
    return high, low


def dot(first, second):
    return jnp.dot(first, second, preferred_element_type=F32)


def dot3(first_high, first_low, second_high, second_low):
    first = jnp.concatenate([first_high, first_high, first_low], axis=1)
    return dot(first, jnp.concatenate([second_high, second_low, second_high], axis=0))


class Ring:
    def __init__(self, block, landing, send, recv, me, right, left):
        def copy(m):
            source, device = self.routes[m]
            return pltpu.make_async_remote_copy(
                src_ref=source,
                dst_ref=landing(m),
                send_sem=send(m),
                recv_sem=recv(m),
                device_id=device,
                device_id_type=MESH,
            )

        opposite, after, before = (lax.rem(me + n, 4) for n in (2, 1, 3))
        self.after, self.before = block(after, 0), block(before, 1)
        self.landing = landing
        self.mine = (block(me, 0), block(me, 1))
        self.copy = copy
        self.routes = (
            (block(opposite, 0), right),
            (block(opposite, 1), left),
            (block(after, 1), right),
            (block(before, 0), left),
            (self.after, right),
            (self.before, left),
        )

    def start(self, *messages):
        for m in messages:
            self.copy(m).start()

    def forward_right(self):
        self.copy(0).wait_recv()
        self.after[...] = self.after[...] + self.landing(0)[...]
        self.copy(4).start()

    def forward_left(self):
        self.copy(1).wait_recv()
        self.before[...] = self.before[...] + self.landing(1)[...]
        self.copy(5).start()

    def forward(self):
        self.forward_right()
        self.forward_left()

    def total(self, half):
        left, right = ((4, 3), (2, 5))[half]
        self.copy(left).wait_recv()
        self.copy(right).wait_recv()
        return self.mine[half][...] + self.landing(left)[...] + self.landing(right)[...]

    def drain(self):
        for m in range(6):
            self.copy(m).wait_send()


class Direct:
    def __init__(self, block, landing, send, recv, me, devices):
        self.mine, self.landing = block(me), landing

        def copy(m):
            return pltpu.make_async_remote_copy(
                src_ref=block(lax.rem(me + (1, 3, 2)[m], 4)),
                dst_ref=landing(m),
                send_sem=send(m),
                recv_sem=recv(m),
                device_id=devices[m],
                device_id_type=MESH,
            )

        self.copy = copy

    def start(self, *messages):
        for m in messages:
            self.copy(m).start()

    def total(self):
        for m in range(3):
            self.copy(m).wait_recv()
        return (self.mine[...] + self.landing(0)[...]) + (self.landing(1)[...] + self.landing(2)[...])

    def drain(self):
        for m in range(3):
            self.copy(m).wait_send()


def kernel(
    psi_hbm, ham_hbm, rot_hbm, over_ref, proj_ref, rotated_hbm,
    raw_a, raw_b, pair_a, pair_b, ah, al, bh, bl, ath, atl,
    rot_buf, out_buf,
    da, db, dc, xa1, xb1, xc1, ea, eb, ec, xa2, xb2, xb2_last, xc2, fa, fb, fc, xa3, xb3, xc3, piece, final,
    sa1, ra1, sb1, rb1, sc1, rc1, s2, r2, s_pair, r_pair, s_fin, r_fin, load_sem, rot_sem, out_sem,
):
    row, col = lax.axis_index("row"), lax.axis_index("col")
    x, core = row // 2, lax.rem(row, 2)
    y, z = col // 4, lax.rem(col, 4)

    def chip(dx=0, dy=0, dz=0):
        return (
            2 * lax.rem(x + dx, 4) + core,
            4 * lax.rem(y + dy, 4) + lax.rem(z + dz, 4),
        )

    partner = (2 * x + 1 - core, col)
    x_right, x_left = chip(dx=1), chip(dx=3)
    y_right, y_left = chip(dy=1), chip(dy=3)
    z_right, z_left = chip(dz=1), chip(dz=3)

    load_a = pltpu.make_async_copy(psi_hbm, raw_a, load_sem.at[0])
    load_b = pltpu.make_async_copy(ham_hbm, raw_b, load_sem.at[1])
    load_a.start()
    load_b.start()
    barrier = pltpu.get_barrier_semaphore()
    for device in (partner, x_right, x_left, y_right, y_left, z_right, z_left):
        pl.semaphore_signal(barrier, inc=1, device_id=device, device_id_type=MESH)

    def rot_load(n):
        slot = lax.rem(n, 2)
        columns = pl.ds(pl.multiple_of(n * CHUNK, CHUNK), CHUNK)
        return pltpu.make_async_copy(rot_hbm.at[:, columns], rot_buf.at[slot], rot_sem.at[slot])

    def rotated_store(n):
        slot = lax.rem(n, 2)
        columns = pl.ds(pl.multiple_of(n * CHUNK, CHUNK), CHUNK)
        return pltpu.make_async_copy(out_buf.at[slot], rotated_hbm.at[:, columns], out_sem.at[slot])

    def block_of(step):
        return lax.rem(x + 2 + 3 * step + 3 * (step // 2) + 2 * (step // 3), 4)

    def cut(start, width):
        return pl.ds(pl.multiple_of(start, width), width)

    def prepare(raw, high, low, base, columns):
        h, l = split(raw[:, columns])
        high[base : base + ROWS, columns] = h
        low[base : base + ROWS, columns] = l

    load_a.wait()

    @pl.loop(0, 8)
    def _(j):
        prepare(raw_a, ah, al, 0, cut(j * 256, 256))

    load_b.wait()

    @pl.loop(0, 4)
    def _(j):
        prepare(raw_b, bh, bl, 0, cut(j * 512, 512))

    pl.semaphore_wait(barrier, 7)

    y_order = (2, 1, 3, 0)

    def pair_copy(source, target, columns, n):
        return pltpu.make_async_remote_copy(
            src_ref=source.at[:, columns],
            dst_ref=target.at[:, columns],
            send_sem=s_pair.at[n],
            recv_sem=r_pair.at[n],
            device_id=partner,
            device_id_type=MESH,
        )

    def a_columns(first, j):
        return cut(lax.rem(first + j, 8) * 256, 256)

    def b_columns(i):
        return cut(lax.rem(y + y_order[i], 4) * 512, 512)

    def pair_a_copy(first, j):
        return pair_copy(psi_hbm, pair_a, a_columns(first, j), j)

    def pair_b_copy(i):
        return pair_copy(ham_hbm, pair_b, b_columns(i), 8 + i)

    first = 2 * block_of(0) + core
    theirs = 2 * block_of(0) + 1 - core
    pair_a_copy(theirs, 0).start()
    pair_a_copy(theirs, 4).start()
    pair_b_copy(0).start()
    pair_b_copy(1).start()
    for j in (1, 2, 3):
        pair_a_copy(theirs, j).start()
    for i in (2, 3):
        pair_b_copy(i).start()
    for j in (5, 6, 7):
        pair_a_copy(theirs, j).start()
    rot_load(0).start()
    rot_load(1).start()

    def take_a(j):
        pair_a_copy(first, j).wait_recv()
        prepare(pair_a, ah, al, ROWS, a_columns(first, j))

    def take_b(i):
        pair_b_copy(i).wait_recv()
        prepare(pair_b, bh, bl, ROWS, b_columns(i))

    def turn(columns):
        for raw, base in ((raw_a, 0), (pair_a, ROWS)):
            h, l = split(raw[:, columns].T)
            ath[:, base : base + ROWS] = h
            atl[:, base : base + ROWS] = l

    def rotated_chunk(n):
        slot = lax.rem(n, 2)
        rot_load(n).wait()
        acc = jnp.zeros((ROWS, CHUNK), F32)
        for k in range(8):
            h, l = split(rot_buf[slot, 256 * k : 256 * k + 256, :])
            part = slice(256 * k, 256 * k + 256)
            acc = acc + dot3(ah[0:ROWS, part], al[0:ROWS, part], h, l)

        @pl.when(n >= 2)
        def _():
            rotated_store(n - 2).wait()

        out_buf[slot] = acc
        rotated_store(n).start()

        @pl.when(n + 2 < M // CHUNK)
        def _():
            rot_load(n + 2).start()

    y_off = ((2, 1), (3, 0))

    def ring_a1(n):
        s, pair = n // 2, n % 2
        return Ring(
            lambda u, h: da.at[u, lax.rem(y + y_off[s][h], 4), 2 * pair : 2 * pair + 2],
            lambda m: xa1.at[n, m],
            lambda m: sa1.at[n, m],
            lambda m: ra1.at[n, m],
            x, x_right, x_left,
        )

    def ring_b1(step):
        block = block_of(step)
        return Ring(
            lambda u, h: db.at[block, u, 2 * h : 2 * h + 2],
            lambda m: xb1.at[step, m],
            lambda m: sb1.at[step, m],
            lambda m: rb1.at[step, m],
            y, y_right, y_left,
        )

    def ring_c1(step):
        block = block_of(step)
        return Ring(
            lambda u, h: dc.at[block, u, 2 * h : 2 * h + 2],
            lambda m: xc1.at[step, m],
            lambda m: sc1.at[step, m],
            lambda m: rc1.at[step, m],
            z, z_right, z_left,
        )

    a_rings = [ring_a1(n) for n in range(4)]

    @pl.loop(0, 4)
    def _(step):
        block = block_of(step)
        strip = 2 * block + core
        b_ring, c_ring = ring_b1(step), ring_c1(step)
        opening = step == 0

        def at_opening(*takes):
            @pl.when(opening)
            def _():
                for take, n in takes:
                    take(n)

        def square(j):
            columns = a_columns(strip, j)
            return dot3(ath[...], atl[...], ah[:, columns], al[:, columns])

        def projected(i):
            yy = lax.rem(y + y_order[i], 4)
            columns = b_columns(i)
            acc = dot3(ath[...], atl[...], bh[:, columns], bl[:, columns])
            for t in range(4):
                da[block, yy, t, 0:TILE] = acc[0:TILE, TILE * t : TILE * t + TILE]
                db[block, yy, t, 0:TILE] = acc[TILE:ROWS, TILE * t : TILE * t + TILE]
            s, h = i // 2, i % 2

            @pl.when(step == 0)
            def _():
                for ring in a_rings[2 * s : 2 * s + 2]:
                    ring.start(h)

            @pl.when(step == 2 - h)
            def _():
                for ring in a_rings[2 * s : 2 * s + 2]:
                    ring.start(3 - h)

        at_opening((take_a, 0))
        turn(a_columns(strip, 0))
        at_opening((take_a, 4))
        acc = square(4)
        swap = strip >= 4
        top = jnp.where(swap, acc[0:TILE, TILE:256], acc[0:TILE, 0:TILE]).reshape(2, 4, 16, TILE)
        low = jnp.where(swap, acc[TILE:ROWS, 0:TILE], acc[TILE:ROWS, TILE:256]).reshape(2, 4, 16, TILE)
        for zz in range(4):
            tile = (top, low)[zz // 2][zz % 2]
            da[block, :, zz, TILE:BAND, :] = tile[:, 0:8]
            db[block, :, zz, TILE:BAND, :] = tile[:, 8:16]
        at_opening((take_b, 0))
        projected(0)
        b_ring.start(0, 1)
        at_opening((take_b, 1))
        projected(1)
        b_ring.start(2)
        at_opening((take_a, 1), (take_a, 2), (take_a, 3))
        for j in range(4):
            acc = square(j)
            for h in range(2):
                t = 2 * j + h
                tile = acc[:, TILE * h : TILE * h + TILE].reshape(4, 4, 16, TILE)
                dc[block, :, :, 16 * t : 16 * t + 16, :] = tile
        c_ring.start(0, 1, 2, 3)
        at_opening((take_b, 2))
        projected(2)
        b_ring.start(3)
        at_opening((take_b, 3))
        projected(3)
        at_opening((take_a, 5), (take_a, 6), (take_a, 7))

        @pl.when(step >= 1)
        def _():
            ring_c1(step - 1).forward()
            ring_b1(step - 1).forward()

        @pl.when(step == 2)
        def _():
            a_rings[0].forward()
            a_rings[1].forward()

    def ring_n(block, landing, sems, me, right, left):
        send, recv = sems
        return Ring(block, landing, lambda m: send.at[m], lambda m: recv.at[m], me, right, left)

    def sems(n):
        return s2.at[n], r2.at[n]

    def in_band(ref, *index):
        return lambda u, h: ref.at[(*index, u, pl.ds(*CUTS[h]))]

    def band_landing(ref, *index):
        return lambda m: ref.at[(*index, m, pl.ds(0, CUTS[HALF[m]][1]))]

    ring_a2 = ring_n(lambda u, h: ea.at[u, 2 * h : 2 * h + 2], lambda m: xa2.at[m], sems(0), y, y_right, y_left)
    ring_c2 = ring_n(lambda u, h: ec.at[u, 2 * h : 2 * h + 2], lambda m: xc2.at[m], sems(1), x, x_right, x_left)
    b2_rings = [
        ring_n(in_band(eb, n), band_landing(xb2, n), sems(2 + n), z, z_right, z_left) for n in range(3)
    ]

    def direct_n(block, landing, n, me, devices):
        return Direct(block, lambda m: landing.at[m], lambda m: s2.at[n, m], lambda m: r2.at[n, m], me, devices)

    x_devices = (x_right, x_left, chip(dx=2))
    y_devices = (y_right, y_left, chip(dy=2))
    z_devices = (z_right, z_left, chip(dz=2))
    b2_last = direct_n(lambda u: eb.at[3, u], xb2_last, 5, z, z_devices)
    ring_a3 = direct_n(lambda u: fa.at[u], xa3, 6, z, z_devices)
    ring_b3 = direct_n(lambda u: fb.at[u], xb3, 7, x, x_devices)
    ring_c3 = direct_n(lambda u: fc.at[u], xc3, 8, y, y_devices)

    def total_b1(n):
        ring = ring_b1(n)
        for h in range(2):
            eb[n, 2 * h : 2 * h + 2] = ring.total(h)
        if n < 3:
            b2_rings[n].start(0, 1, 2, 3)
        else:
            b2_last.start(2, 0, 1)

    def total_c1(n):
        ring = ring_c1(n)
        for h in range(2):
            ec[block_of(n), 2 * h : 2 * h + 2] = ring.total(h)
        ring_c2.start(*OPENINGS[n])

    def total_a1(s, h):
        for n in range(2):
            ea[lax.rem(y + y_off[s][h], 4), 2 * n : 2 * n + 2] = a_rings[2 * s + n].total(h)
        ring_a2.start(*OPENINGS[2 * s + h])

    def total_b2(n):
        if n == 3:
            fb[block_of(n)] = b2_last.total()
            return
        for h in range(2):
            start, size = CUTS[h]
            fb[block_of(n), start : start + size] = b2_rings[n].total(h)
        ring_b3.start((2, 0, 1)[n])

    def total_2(ring, ref, then):
        for h in range(2):
            ref[2 * h : 2 * h + 2] = ring.total(h)
        then.start(2, 0, 1)

    def total_c3():
        piece[0:TILE] = ring_c3.total()
        for finish in finishes[:8]:
            finish.start()

    def total_3(ring, base, rest):
        total = ring.total()
        proj_ref[base : base + TILE, :] = total[0:TILE] * scale
        piece[rest : rest + 8] = total[TILE:BAND]

    scale = 1.0 / (ROWS * 128)
    strip = row
    part = 4 * z + y
    part_half, part_rest = part // 8, lax.rem(part, 8)
    slot = pl.ds(pl.multiple_of(16 * part_rest, 16), 16)

    class Finish:
        def __init__(self, t):
            self.t, self.source = t, piece.at[16 * t : 16 * t + 16]
            self.other = lax.rem(strip + t // 2, 8)
            self.side = t % 2 if t < 8 else lax.rem(part_half + strip // 4, 2)
            self.target = 2 * self.other + self.side

        def copy(self, n, device, place):
            return pltpu.make_async_remote_copy(
                src_ref=self.source,
                dst_ref=place,
                send_sem=s_fin.at[n],
                recv_sem=r_fin.at[0],
                device_id=device,
                device_id_type=MESH,
            )

        def direct(self):
            return self.copy(self.t, (strip, self.target), final.at[part_half, slot])

        def mirror(self):
            return self.copy(7 + self.t, (self.other, 2 * strip + part_half), final.at[self.side, slot])

        def start(self):
            stay = pltpu.make_async_copy(self.source, final.at[part_half, slot], r_fin.at[0])
            direct = self.direct()
            pl.when(self.target != col)(direct.start)
            pl.when(self.target == col)(stay.start)
            if self.t >= 2:
                self.mirror().start()

        def drain(self):
            pl.when(self.target != col)(self.direct().wait_send)
            if self.t >= 2:
                self.mirror().wait_send()

    finishes = [Finish(t) for t in range(9)]

    a_rings[2].forward_right()
    a_rings[3].forward_right()
    total_c1(0)
    pl.loop(0, 3)(rotated_chunk)
    total_c1(1)
    a_rings[2].forward_left()
    ring_b1(3).forward_right()
    total_b1(1)
    ring_c1(3).forward_right()
    total_b1(0)
    ring_c1(3).forward_left()
    total_a1(0, 0)
    ring_b1(3).forward_left()
    total_a1(0, 1)
    pl.loop(3, 5)(rotated_chunk)
    total_c1(2)
    b2_rings[1].forward_right()
    b2_rings[1].forward_left()
    ring_c2.forward_left()
    a_rings[3].forward_left()
    total_b1(2)
    total_a1(1, 0)
    b2_rings[0].forward_left()
    ring_a2.forward_left()
    pl.loop(5, 6)(rotated_chunk)
    ring_c2.forward_right()
    b2_rings[0].forward_right()
    ring_a2.forward_right()
    pl.loop(6, 7)(rotated_chunk)
    total_c1(3)
    b2_rings[2].forward_left()
    b2_rings[2].forward_right()
    total_b1(3)
    total_b2(1)
    pl.loop(7, 8)(rotated_chunk)
    total_b2(0)
    total_2(ring_c2, fc, ring_c3)
    total_b2(2)
    total_a1(1, 1)
    total_2(ring_a2, fa, ring_a3)
    total_b2(3)
    total_3(ring_b3, TILE, 136)
    total_c3()
    total_3(ring_a3, 0, 128)
    finishes[8].start()

    for n in range(12):
        (pair_a_copy(theirs, n) if n < 8 else pair_b_copy(n - 8)).wait_send()
    for ring in a_rings:
        ring.drain()

    @pl.loop(0, 4)
    def _(step):
        ring_b1(step).drain()
        ring_c1(step).drain()

    for ring in (ring_a2, ring_c2, *b2_rings, b2_last, ring_a3, ring_b3, ring_c3):
        ring.drain()
    rotated_store(M // CHUNK - 2).wait()
    rotated_store(M // CHUNK - 1).wait()

    pltpu.make_async_copy(final, final, r_fin.at[0]).wait()
    other, side = col // 2, lax.rem(col, 2)
    distance = lax.rem(other - strip + 8, 8)
    for h in range(2):
        straight = (distance < 4) | ((distance == 4) & (lax.rem(side + strip // 4, 2) == h))
        tile = final[h]
        over_ref[TILE * h : TILE * h + TILE, :] = jnp.where(straight, tile, tile.T) * scale
    for finish in finishes:
        finish.drain()


def hand_on(over_in, proj_in, rotated_in, over_out, proj_out, rotated_out, over, proj, rotated, load, store):
    moves = [(over_in, over, over_out), (proj_in, proj, proj_out)]
    for n in range(4):
        rows = pl.ds(64 * n, 64)
        moves.append((rotated_in.at[rows], rotated.at[rows], rotated_out.at[rows]))
    loads = [pltpu.make_async_copy(a, b, load.at[n]) for n, (a, b, _) in enumerate(moves)]
    stores = [pltpu.make_async_copy(b, c, store.at[n]) for n, (_, b, c) in enumerate(moves)]
    for copy in loads:
        copy.start()
    for first, second in zip(loads, stores):
        first.wait()
        second.start()
    for copy in stores:
        copy.wait()


def local(filtered, hamiltonian_applied, rotation):
    vmem = pltpu.VMEM
    dma = pltpu.SemaphoreType.DMA
    any_spec = pl.BlockSpec(memory_space=pl.ANY)
    vmem_spec = pl.BlockSpec(memory_space=pltpu.VMEM)
    flops = 3 * 2 * ROWS * M * M * 3
    shapes = (
        jax.ShapeDtypeStruct((256, TILE), F32),
        jax.ShapeDtypeStruct((256, TILE), F32),
        jax.ShapeDtypeStruct((ROWS, M), F32),
    )
    made = pl.pallas_call(
        kernel,
        out_shape=shapes,
        in_specs=[any_spec] * 3,
        out_specs=(vmem_spec, vmem_spec, any_spec),
        scratch_shapes=[
            vmem((ROWS, M), F32), vmem((ROWS, M), F32), vmem((ROWS, M), F32), vmem((ROWS, M), F32),
            vmem((512, M), BF16), vmem((512, M), BF16), vmem((512, M), BF16), vmem((512, M), BF16),
            vmem((256, 512), BF16), vmem((256, 512), BF16),
            vmem((2, M, CHUNK), F32), vmem((2, ROWS, CHUNK), F32),
            vmem((4, 4, 4, BAND, TILE), F32), vmem((4, 4, 4, BAND, TILE), F32), vmem((4, 4, 4, TILE, TILE), F32),
            vmem((4, 6, 2, BAND, TILE), F32), vmem((4, 6, 2, BAND, TILE), F32), vmem((4, 6, 2, TILE, TILE), F32),
            vmem((4, 4, BAND, TILE), F32), vmem((4, 4, BAND, TILE), F32), vmem((4, 4, TILE, TILE), F32),
            vmem((6, 2, BAND, TILE), F32), vmem((3, 6, 72, TILE), F32), vmem((3, BAND, TILE), F32), vmem((6, 2, TILE, TILE), F32),
            vmem((4, BAND, TILE), F32), vmem((4, BAND, TILE), F32), vmem((4, TILE, TILE), F32),
            vmem((3, BAND, TILE), F32), vmem((3, BAND, TILE), F32), vmem((3, TILE, TILE), F32),
            vmem((144, TILE), F32), vmem((2, TILE, TILE), F32),
            dma((4, 6)), dma((4, 6)), dma((4, 6)), dma((4, 6)), dma((4, 6)), dma((4, 6)),
            dma((9, 6)), dma((9, 6)),
            dma((12,)), dma((12,)), dma((16,)), dma((1,)), dma((2,)), dma((2,)), dma((2,)),
        ],
        compiler_params=pltpu.CompilerParams(
            collective_id=0, has_side_effects=True, vmem_limit_bytes=62 << 20
        ),
        cost_estimate=pl.CostEstimate(flops=flops, bytes_accessed=24 << 20, transcendentals=0),
    )(filtered, hamiltonian_applied, rotation)
    return pl.pallas_call(
        hand_on,
        out_shape=shapes,
        in_specs=[any_spec] * 3,
        out_specs=(any_spec,) * 3,
        scratch_shapes=[vmem((256, TILE), F32), vmem((256, TILE), F32), vmem((ROWS, M), F32), dma((6,)), dma((6,))],
    )(*made)


def solution(mesh):
    return jax.shard_map(
        local,
        mesh=mesh,
        in_specs=(P(("row", "col"), None), P(("row", "col"), None), P()),
        out_specs=(P("row", "col"), P("row", "col"), P(("row", "col"), None)),
        check_vma=False,
    )
```
